32 devices in a mesh: ka: 16 (over z, y, core), freq: 2 (over x).
Axes of the slice: x: 2, y: 2, z: 4, core: 2. Of those that a mesh axis runs over, the one named last changes fastest.
Arguments:
- energy: float32 [16, 128], P('ka'), may hold values from -2.4 to 2.4, as said below
- projector: float32 [16, 2, 128, 40], P('ka'), may hold values from -0.25 to 0.25
- self_energy: float32 [32, 2, 40, 40], P('freq'), may hold values from -0.5 to 0.5
- multiplicity: int32 [16], P('ka'), may hold values from 1 to 5
- orbitals: float32 [16, 2, 128, 16, 256], P('ka', None, None, None, 'freq'), may hold values from -12 to 12
- owner: int32 [16], replicated, may hold values from 0 to 15, each once
- rotation: float32 [40, 40], replicated, may hold values from -1 to 1
Outputs:
- local_green: float32 [32, 2, 40, 40], P('freq')
- slab_charge: float32 [16, 256], P('ka', 'freq')
The draws below stay inside these ranges and needn't reach their ends.
Inputs may be any that keep to these rules, and one draw needn't show every extreme that they name: Every band energy has a magnitude between 1.6 and 2.4. `owner`: each ka index owns exactly one slab.
All inputs are finite; a program needn't handle non-finite values.
Results may differ from the reference program's by a relative error of at most 0.0001.
Values sent between devices are 32-bit elements; how exact they have to be, the bound alone decides.
A program may use at most 64 MiB of HBM per device.

```python
import math
import jax
import jax.numpy as jnp
from jax import lax

NB = 128
NO = 40
F_DEV = 16
NS_STEPS = 3
KPTS = 16
FERMION_POLES = 32
SLABS = 16
SLAB_PTS = 256


def draw_energy(key, part):
    sign_key, size_key = jax.random.split(jax.random.fold_in(key, 43))
    quarter = jax.random.randint(sign_key, (KPTS, NB), 0, 4)
    sign = jnp.where(quarter < 3, -1.0, 1.0).astype(jnp.float32)
    spread = jax.random.uniform(size_key, (KPTS, NB), jnp.float32, 0.0, 1.0)
    magnitude = 1.6 + 0.8 * spread
    return (sign * magnitude).astype(jnp.float32)


def draw_multiplicity(key, part):
    random_part = jax.random.randint(jax.random.fold_in(key, 11), (KPTS,), 1, 3)
    rising = 4 * jnp.arange(KPTS, dtype=jnp.int32) // KPTS
    return (random_part + rising).astype(jnp.int32)


def draw_self_energy(key, part):
    shift_key, damp_key, couple_key = jax.random.split(jax.random.fold_in(key, 29), 3)
    off_diagonal = 1.0 - jnp.eye(NO, dtype=jnp.float32)
    coupling = jax.random.truncated_normal(couple_key, -3.0, 3.0, (FERMION_POLES, 2, NO, NO), jnp.float32)
    damping = jnp.exp(jax.random.uniform(damp_key, (FERMION_POLES, NO), jnp.float32, math.log(0.05), math.log(0.5)))
    shifting = jax.random.uniform(shift_key, (FERMION_POLES, NO), jnp.float32, -0.4, 0.4)
    coupling = coupling * (0.12 / math.sqrt(NO)) * off_diagonal
    diagonal = jnp.stack([shifting, -damping], axis=1)[:, :, :, None] * jnp.eye(NO, dtype=jnp.float32)
    return (coupling + diagonal).astype(jnp.float32)


def steps_of(rng, dims, cuts, smallest, top_value):
    loudness, own = 1.0, jax.random.fold_in(rng, 6)
    for axis_at, shards_of in cuts:
        draws = jnp.exp(jax.random.uniform(jax.random.fold_in(own, axis_at), (shards_of,), jnp.float32, smallest / len(cuts), top_value / len(cuts)))
        loudness = loudness * jnp.repeat(draws, dims[axis_at] // shards_of).reshape([-1 if axis == axis_at else 1 for axis in range(len(dims))])
    return loudness


def gaussian(own_key, shape, scale, limit, pieces=(), held_as=jnp.bfloat16):
    drawn = scale * jax.random.normal(own_key, shape, jnp.float32)
    if pieces:
        drawn = drawn * steps_of(own_key, shape, pieces, -0.22, 0.18)
    return jnp.clip(drawn, -limit, limit).astype(held_as)


def setup_inputs(seed: int = 0) -> dict:
    key_list = jax.random.split(jax.random.key(seed), 8)
    return {
        "energy": draw_energy(jax.random.fold_in(key_list[7], 71), 0),
        "projector": gaussian(key_list[1], (KPTS, 2, NB, NO), (4 * NB) ** -0.5, 0.25, ((0, 16),), jnp.float32),
        "self_energy": draw_self_energy(jax.random.fold_in(key_list[7], 71), 0),
        "multiplicity": draw_multiplicity(jax.random.fold_in(key_list[7], 71), 0),
        "orbitals": gaussian(key_list[4], (KPTS, 2, NB, SLABS, SLAB_PTS), 2.0, 12.0, ((0, 16), (4, 2)), jnp.float32),
        "owner": jax.random.permutation(key_list[5], SLABS).astype(jnp.int32),
        "rotation": gaussian(key_list[6], (NO, NO), NO ** -0.5, 1.0, (), jnp.float32),
    }


PRECISE = lax.Precision.HIGHEST


def complex_product(first_pair, second_pair, formula):
    direct = jnp.einsum(formula, first_pair[0], second_pair[0], precision=PRECISE)
    opposed = jnp.einsum(formula, first_pair[1], second_pair[1], precision=PRECISE)
    mixed_one = jnp.einsum(formula, first_pair[0], second_pair[1], precision=PRECISE)
    mixed_two = jnp.einsum(formula, first_pair[1], second_pair[0], precision=PRECISE)
    return (direct - opposed, mixed_one + mixed_two)


def complex_times(first_pair, second_pair):
    return (first_pair[0] * second_pair[0] - first_pair[1] * second_pair[1],
            first_pair[0] * second_pair[1] + first_pair[1] * second_pair[0])


def green_block(energy_row, projector_pair, self_pair, pole_location):
    band_count = energy_row.shape[0]
    identity = jnp.eye(band_count, dtype=jnp.float32)
    squared = pole_location[:, None] * pole_location[:, None] + energy_row[None, :] * energy_row[None, :]
    bare_real = -energy_row[None, :] / squared
    bare_imag = -pole_location[:, None] / squared
    rightward_scale = (bare_real[:, None, :], bare_imag[:, None, :])
    row_side = (bare_real[:, :, None], bare_imag[:, :, None])
    adjoint = (projector_pair[0].T, -projector_pair[1].T)
    folded = complex_product(self_pair, adjoint, "fab,bj->faj")
    upfold = complex_product(projector_pair, folded, "ia,faj->fij")
    sandwich = complex_times(row_side, complex_times(upfold, rightward_scale))
    reciprocal_operator = (identity * rightward_scale[0] + sandwich[0], identity * rightward_scale[1] + sandwich[1])
    for repeat in range(NS_STEPS - 1):
        reduced = complex_product(adjoint, reciprocal_operator, "aj,fjk->fak")
        coupled = complex_product(self_pair, reduced, "fab,fbk->fak")
        lifted = complex_product(projector_pair, coupled, "ia,fak->fik")
        shift_real = -energy_row[None, :, None] * reciprocal_operator[0] - pole_location[:, None, None] * reciprocal_operator[1]
        shift_imag = -energy_row[None, :, None] * reciprocal_operator[1] + pole_location[:, None, None] * reciprocal_operator[0]
        residue = (identity - shift_real + lifted[0], lifted[1] - shift_imag)
        update = complex_product(reciprocal_operator, residue, "fij,fjk->fik")
        reciprocal_operator = (reciprocal_operator[0] + update[0], reciprocal_operator[1] + update[1])
    return reciprocal_operator, rightward_scale


def electron_filling(reciprocal_operator, rightward_scale, thermal_level):
    band_count = reciprocal_operator[0].shape[1]
    identity = jnp.eye(band_count, dtype=jnp.float32)
    excess_inphase = jnp.sum(reciprocal_operator[0] - identity * rightward_scale[0], axis=0)
    excess_quadrature = jnp.sum(reciprocal_operator[1] - identity * rightward_scale[1], axis=0)
    return (thermal_level * (excess_inphase + excess_inphase.T), thermal_level * (excess_quadrature - excess_quadrature.T))


def project_local(reciprocal_operator, projector_pair):
    adjoint = (projector_pair[0].T, -projector_pair[1].T)
    reduced = complex_product(adjoint, reciprocal_operator, "aj,fjk->fak")
    return complex_product(reduced, projector_pair, "fak,kb->fab")


def slab_density(orbital_filling_table, orbital_set):
    top_rows = jnp.concatenate([orbital_filling_table[0], -orbital_filling_table[1]], axis=1)
    bottom_rows = jnp.concatenate([orbital_filling_table[1], orbital_filling_table[0]], axis=1)
    realified = jnp.concatenate([top_rows, bottom_rows], axis=0)
    columns = orbital_set.reshape(realified.shape[0], -1)
    product = jnp.dot(realified, columns, precision=PRECISE, preferred_element_type=jnp.float32)
    return jnp.sum(columns * product, axis=0)


def reference(energy, projector, self_energy, multiplicity, orbitals, owner, rotation):
    thermal_level = 0.25 / FERMION_POLES
    slot_index = jnp.arange(FERMION_POLES, dtype=jnp.int32)
    fermionic_poles = (slot_index % F_DEV) * (FERMION_POLES // F_DEV) + slot_index // F_DEV
    pole_location = (2 * fermionic_poles + 1).astype(jnp.float32) * (math.pi * thermal_level)
    self_pair = (self_energy[:, 0], self_energy[:, 1])

    def accumulate(running, inputs):
        local_real, local_imag, charge = running
        energy_row, projector_one, multiple, orbital_set = inputs
        projector_pair = (projector_one[0], projector_one[1])
        reciprocal_operator, rightward_scale = green_block(energy_row, projector_pair, self_pair, pole_location)
        weight = multiple.astype(jnp.float32)
        projected = project_local(reciprocal_operator, projector_pair)
        orbital_filling_table = electron_filling(reciprocal_operator, rightward_scale, thermal_level)
        charge = charge + weight * slab_density(orbital_filling_table, orbital_set)
        return (local_real + weight * projected[0], local_imag + weight * projected[1], charge), None

    initial = (jnp.zeros((FERMION_POLES, NO, NO), jnp.float32), jnp.zeros((FERMION_POLES, NO, NO), jnp.float32),
               jnp.zeros((SLABS * SLAB_PTS,), jnp.float32))
    finals, unused = lax.scan(accumulate, initial, (energy, projector, multiplicity, orbitals))
    local_real, local_imag, charge = finals
    weight_total = jnp.sum(multiplicity.astype(jnp.float32))
    stacked = jnp.stack([local_real, local_imag]) / weight_total
    turned = jnp.einsum("pfbc,cd->pfbd", stacked, rotation, precision=PRECISE)
    rotated = jnp.einsum("ba,pfbd->pfad", rotation, turned, precision=PRECISE)
    local_green = jnp.transpose(rotated, (1, 0, 2, 3))
    slab_rows = charge.reshape(SLABS, SLAB_PTS) / weight_total
    selector = (owner[None, :] == jnp.arange(SLABS, dtype=jnp.int32)[:, None]).astype(jnp.float32)
    slab_charge = jnp.dot(selector, slab_rows, precision=PRECISE)
    return local_green, slab_charge
```

```python
import functools
import math

import jax
import jax.numpy as jnp
from jax import lax
from jax.experimental import pallas as pl
from jax.experimental.pallas import tpu as pltpu
from jax.sharding import PartitionSpec as P

NS_STEPS = 3
GROUP = 8
HALF = 64
F32 = jnp.float32
BF16 = jnp.bfloat16
MESH = pl.DeviceIdType.MESH


def split(value):
    high = value.astype(BF16)
    return high, (value - high.astype(F32)).astype(BF16)


def dot3(first, second):
    one = functools.partial(jnp.dot, preferred_element_type=F32)
    return one(first[0], second[0]) + (one(first[1], second[0]) + one(first[0], second[1]))


def exact_dot(first, second):
    return jnp.dot(first, second, precision=lax.Precision.HIGHEST, preferred_element_type=F32)


def lanes(shape):
    return lax.broadcasted_iota(jnp.int32, shape, len(shape) - 1)


def rows(shape):
    return lax.broadcasted_iota(jnp.int32, shape, 0)


def swap(pair):
    turned = pltpu.roll(pair, HALF, 1)
    return jnp.where(lanes(pair.shape) < HALF, -turned, turned)


def tall(top, bottom):
    gap = jnp.zeros((HALF - top.shape[0], top.shape[1]), F32)
    return jnp.concatenate([top, gap, bottom, gap], axis=0)


def packed(real, imag):
    gap = jnp.zeros((real.shape[0], HALF - real.shape[1]), F32)
    return jnp.concatenate([real, gap, imag, gap], axis=1)


def green_kernel(thermal, mult_ref, energy_ref, proj_ref, self_ref, density_ref, local_ref, total_ref):
    slots, orbs = self_ref.shape[0], self_ref.shape[2]
    bands = energy_ref.shape[1]
    freq_count, freq_at = lax.axis_size("freq"), lax.axis_index("freq")
    weight = mult_ref[0].astype(F32)
    pair = packed(proj_ref[0, 0], proj_ref[0, 1])
    swapped = swap(pair)
    across = jnp.transpose(pair)
    across_re, across_im = across[:orbs], across[HALF : HALF + orbs]
    weights_pp = split(jnp.concatenate([pair, swapped], axis=0))
    energy = energy_ref[...]
    energy_col = jnp.transpose(jnp.broadcast_to(energy, (bands, bands)))
    lane = lanes((orbs, 2 * HALF))
    unit = jnp.where(lane == rows((orbs, 2 * HALF)), 1.0, 0.0).astype(F32)
    total_ref[...] = jnp.zeros_like(total_ref)

    def body(step, carry):
        at = [step * GROUP + g for g in range(GROUP)]
        omega = [(2 * (q * freq_count + freq_at) + 1).astype(F32) * (math.pi * thermal) for q in at]
        inv = [1.0 / (w * w + energy * energy) for w in omega]
        bare_re = [-energy * v for v in inv]
        bare_im = [-w * v for w, v in zip(omega, inv)]
        c_re = [across_re * r + across_im * i for r, i in zip(bare_re, bare_im)]
        c_im = [across_re * i - across_im * r for r, i in zip(bare_re, bare_im)]
        g = [dot3(split(jnp.concatenate([a, b], axis=1)), weights_pp) for a, b in zip(c_re, c_im)]
        s = [split(packed(self_ref[q, 0], self_ref[q, 1])) for q in at]
        first = [
            split(tall(jnp.concatenate([a, b, c], axis=1), jnp.concatenate([-b, a, swap(c)], axis=1)))
            for a, b, c in zip(c_re, c_im, g)
        ]
        out = [dot3(a, b) for a, b in zip(s, first)]
        sc_re = [o[:, :bands] for o in out]
        sc_im = [o[:, bands : 2 * bands] for o in out]
        a1 = [o[:, 2 * bands :] for o in out]
        real_a = [split(tall(a, swap(a))) for a in a1]
        a2 = [dot3(split(a), r) for a, r in zip(a1, real_a)]
        a3 = [dot3(split(a), r) for a, r in zip(a2, real_a)]
        h = [a + b + c for a, b, c in zip(a1, a2, a3)]
        poly = [unit + a + dot3(split(a), split(tall(b, swap(b)))) for a, b in zip(h, a3)]
        real_sc = [
            split(tall(jnp.concatenate([a, b], axis=1), jnp.concatenate([-b, a], axis=1)))
            for a, b in zip(sc_re, sc_im)
        ]
        poly = [split(p) for p in poly]
        v = [dot3(p, r) for p, r in zip(poly, real_sc)]
        wg = [dot3(p, r) for p, r in zip(poly, real_a)]
        for q, one_g, one_w in zip(at, g, wg):
            one = weight * (one_g + dot3(split(one_g), split(tall(one_w, swap(one_w)))))
            local_ref[q] = jnp.where(lane >= HALF + orbs, weight, one)
        gain = None
        for w, one_v in zip(omega, v):
            inv_col = 1.0 / (w * w + energy_col * energy_col)
            left = split(pair * (-energy_col * inv_col) + swapped * (-w * inv_col))
            v_re, v_im = one_v[:, :bands], one_v[:, bands:]
            right = split(tall(one_v, jnp.concatenate([-v_im, v_re], axis=1)))
            term = dot3(left, right)
            gain = term if gain is None else gain + term
        total_ref[...] += gain
        return carry

    lax.fori_loop(0, slots // GROUP, body, 0)
    e_re, e_im = total_ref[:, :bands], total_ref[:, bands:]
    d_re = thermal * (e_re + jnp.transpose(e_re))
    d_im = thermal * (e_im - jnp.transpose(e_im))
    square = (bands, bands)
    density_ref[...] = jnp.where(rows(square) <= lanes(square), d_re, d_im)


def exchange_kernel(
    ka_count, freq_count, mult_ref, owner_ref, density_ref, local_ref, rotation_ref, orbital_ref,
    green_ref, slab_ref,
    columns, high, low, density_in, local_in, mine, gathered, rates, charge_out, charge_in,
    orbital_sem, density_sem, local_sem, gather_sem, charge_sem,
):
    me, freq_me = lax.axis_index("ka"), lax.axis_index("freq")
    slots, orbs, wide = local_ref.shape
    bands = density_ref.shape[0]
    slabs = columns.shape[0] // (2 * bands)
    owners = min(slots, ka_count)
    each = slots // owners

    load = pltpu.make_async_copy(orbital_ref, columns, orbital_sem)
    load.start()

    barrier = pltpu.get_barrier_semaphore()
    for j in range(1, ka_count):
        pl.semaphore_signal(barrier, inc=1, device_id={"ka": lax.rem(me + j, ka_count)}, device_id_type=MESH)
    for j in range(1, freq_count):
        pl.semaphore_signal(
            barrier, inc=1, device_id={"freq": lax.rem(freq_me + j, freq_count)}, device_id_type=MESH
        )
    pl.semaphore_wait(barrier, ka_count + freq_count - 2)

    density_copies = []
    for j in range(1, freq_count):
        density_copies.append(
            pltpu.make_async_remote_copy(
                src_ref=density_ref, dst_ref=density_in.at[j - 1],
                send_sem=density_sem.at[0, j - 1], recv_sem=density_sem.at[1, j - 1],
                device_id={"freq": lax.rem(freq_me + j, freq_count)}, device_id_type=MESH,
            )
        )
        density_copies[-1].start()

    def when_owner(index, action):
        if owners == ka_count:
            action()
        else:
            pl.when(index < owners)(action)

    def chunk(index):
        return pl.ds(index * each, each)

    local_copies = []
    for j in range(1, ka_count):
        to = lax.rem(me + j, ka_count)
        aim = to if owners == ka_count else jnp.minimum(to, owners - 1)
        copy = pltpu.make_async_remote_copy(
            src_ref=local_ref.at[chunk(aim)], dst_ref=local_in.at[j - 1],
            send_sem=local_sem.at[0, j - 1], recv_sem=local_sem.at[1, j - 1],
            device_id={"ka": to}, device_id_type=MESH,
        )
        local_copies.append((copy, to))
        when_owner(to, copy.start)

    load.wait()
    for s in range(slabs):
        one = columns[pl.ds(s, 2 * bands, stride=slabs), :]
        high[s], low[s] = split(one)

    gather_copies = []
    for j in range(1, ka_count):
        to = lax.rem(me + j, ka_count)
        place = me if owners == ka_count else jnp.minimum(me, owners - 1)
        gather_copies.append(
            pltpu.make_async_remote_copy(
                src_ref=mine, dst_ref=gathered.at[chunk(place)],
                send_sem=gather_sem.at[0, j - 1], recv_sem=gather_sem.at[1, j - 1],
                device_id={"ka": to}, device_id_type=MESH,
            )
        )

    def reduce_and_send():
        for copy, _ in local_copies:
            copy.wait_recv()
        turn = rotation_ref[...]
        gap = jnp.zeros((orbs, HALF - orbs), F32)
        zero = jnp.zeros((orbs, HALF), F32)
        right = tall(jnp.concatenate([turn, gap, zero], axis=1), jnp.concatenate([zero, turn, gap], axis=1))
        left = jnp.transpose(turn)
        for e in range(each):
            acc = local_ref[me * each + e]
            for j in range(1, ka_count):
                acc = acc + local_in[j - 1, e]
            share = acc / acc[:1, wide - 1 :]
            mine[e] = exact_dot(left, exact_dot(share, right))
        for copy in gather_copies:
            copy.start()

    when_owner(me, reduce_and_send)
    for copy, to in local_copies:
        when_owner(to, copy.wait_send)

    for copy in density_copies:
        copy.wait()
    density = density_ref[...]
    for j in range(1, freq_count):
        density = density + density_in[j - 1]
    square = (bands, bands)
    row, lane = rows(square), lanes(square)
    upper = jnp.where(row < lane, 2.0 * density, jnp.where(row == lane, density, 0.0))
    lower = jnp.where(row > lane, 2.0 * density, 0.0)
    cross = lower - jnp.transpose(lower)
    form = split(
        jnp.concatenate(
            [
                jnp.concatenate([upper, jnp.zeros(square, F32)], axis=1),
                jnp.concatenate([cross, upper], axis=1),
            ],
            axis=0,
        )
    )
    weight = mult_ref[0].astype(F32)
    for s in range(slabs):
        product = dot3(form, (high[s], low[s]))
        one = high[s].astype(F32) + low[s].astype(F32)
        rates[pl.ds(s, 1), :] = weight * jnp.sum(product * one, axis=0, keepdims=True)
    selector = jnp.where(owner_ref[...] == rows((slabs, slabs)), 1.0, 0.0).astype(F32)
    owned = exact_dot(selector, rates[...])
    for d in range(slabs):
        charge_out[d, 0:1, :] = owned[d : d + 1]
        charge_out[d, 1:2, :] = jnp.full((1, owned.shape[1]), weight, F32)
    charge_copies = []
    for j in range(1, ka_count):
        to = lax.rem(me + j, ka_count)
        copy = pltpu.make_async_remote_copy(
            src_ref=charge_out.at[to], dst_ref=charge_in.at[j - 1],
            send_sem=charge_sem.at[0, j - 1], recv_sem=charge_sem.at[1, j - 1],
            device_id={"ka": to}, device_id_type=MESH,
        )
        copy.start()
        charge_copies.append(copy)

    def store(q, value):
        green_ref[q, 0] = value[:, :orbs]
        green_ref[q, 1] = pltpu.roll(value, HALF, 1)[:, :orbs]

    def own_place():
        for e in range(each):
            store(me * each + e, mine[e])

    for j, copy in enumerate(gather_copies, 1):
        source = lax.rem(me + ka_count - j, ka_count)

        def take(copy=copy, source=source):
            copy.wait_recv()
            for e in range(each):
                store(source * each + e, gathered[source * each + e])

        when_owner(source, take)
    when_owner(me, own_place)

    def sent():
        for copy in gather_copies:
            copy.wait_send()

    when_owner(me, sent)
    for copy in charge_copies:
        copy.wait()
    acc = charge_out[me]
    for j in range(1, ka_count):
        acc = acc + charge_in[j - 1]
    slab_ref[...] = acc[0:1] / acc[1:2]


def local(energy, projector, self_energy, multiplicity, orbitals, owner, rotation):
    slots, orbs = self_energy.shape[0], self_energy.shape[2]
    bands = energy.shape[1]
    slab_count, point_count = orbitals.shape[3], orbitals.shape[4]
    freq_count, ka_count = lax.axis_size("freq"), lax.axis_size("ka")
    thermal = 0.25 / (slots * freq_count)
    vmem = pl.BlockSpec(memory_space=pltpu.VMEM)
    smem = pl.BlockSpec(memory_space=pltpu.SMEM)
    density, local_sum = pl.pallas_call(
        functools.partial(green_kernel, thermal),
        out_shape=(
            jax.ShapeDtypeStruct((bands, bands), F32),
            jax.ShapeDtypeStruct((slots, orbs, 2 * HALF), F32),
        ),
        in_specs=[smem, vmem, vmem, vmem],
        out_specs=(vmem, vmem),
        scratch_shapes=[pltpu.VMEM((bands, 2 * bands), F32)],
        name="green",
    )(multiplicity, energy, projector, self_energy)
    owners = min(slots, ka_count)
    each = slots // owners
    dma = pltpu.SemaphoreType.DMA
    columns = orbitals.reshape(2 * bands * slab_count, point_count)
    return pl.pallas_call(
        functools.partial(exchange_kernel, ka_count, freq_count),
        out_shape=(
            jax.ShapeDtypeStruct((slots, 2, orbs, orbs), F32),
            jax.ShapeDtypeStruct((1, point_count), F32),
        ),
        in_specs=[smem, vmem, vmem, vmem, vmem, pl.BlockSpec(memory_space=pl.ANY)],
        out_specs=(vmem, vmem),
        scratch_shapes=[
            pltpu.VMEM(columns.shape, F32),
            pltpu.VMEM((slab_count, 2 * bands, point_count), BF16),
            pltpu.VMEM((slab_count, 2 * bands, point_count), BF16),
            pltpu.VMEM((max(freq_count - 1, 1), bands, bands), F32),
            pltpu.VMEM((ka_count - 1, each, orbs, 2 * HALF), F32),
            pltpu.VMEM((each, orbs, 2 * HALF), F32),
            pltpu.VMEM((slots, orbs, 2 * HALF), F32),
            pltpu.VMEM((slab_count, point_count), F32),
            pltpu.VMEM((slab_count, 2, point_count), F32),
            pltpu.VMEM((ka_count - 1, 2, point_count), F32),
            dma,
            dma((2, max(freq_count - 1, 1))),
            dma((2, ka_count - 1)),
            dma((2, ka_count - 1)),
            dma((2, ka_count - 1)),
        ],
        compiler_params=pltpu.CompilerParams(collective_id=0, has_side_effects=True),
        name="exchange",
    )(multiplicity, owner.reshape(1, slab_count), density, local_sum, rotation, columns)


def solution(mesh):
    in_specs = (
        P("ka", None),
        P("ka", None, None, None),
        P("freq", None, None, None),
        P("ka"),
        P("ka", None, None, None, "freq"),
        P(),
        P(),
    )
    out_specs = (P("freq", None, None, None), P("ka", "freq"))
    return jax.shard_map(local, mesh=mesh, in_specs=in_specs, out_specs=out_specs, check_vma=False)
```

```python
import functools
import math

import jax
import jax.numpy as jnp
from jax import lax
from jax.experimental import pallas as pl
from jax.experimental.pallas import tpu as pltpu
from jax.sharding import PartitionSpec as P

NS_STEPS = 3
PARTS = 2
HALF = 64
F32 = jnp.float32
BF16 = jnp.bfloat16
MESH = pl.DeviceIdType.MESH


def split(value):
    high = value.astype(BF16)
    return high, (value - high.astype(F32)).astype(BF16)


def dot3(first, second):
    one = functools.partial(jnp.dot, preferred_element_type=F32)
    return one(first[0], second[0]) + (one(first[1], second[0]) + one(first[0], second[1]))


def exact_dot(first, second):
    return jnp.dot(first, second, precision=lax.Precision.HIGHEST, preferred_element_type=F32)


def lanes(shape):
    return lax.broadcasted_iota(jnp.int32, shape, len(shape) - 1)


def rows(shape):
    return lax.broadcasted_iota(jnp.int32, shape, 0)


def swap(pair):
    turned = pltpu.roll(pair, HALF, 1)
    return jnp.where(lanes(pair.shape) < HALF, -turned, turned)


def tall(top, bottom):
    gap = jnp.zeros((HALF - top.shape[0], top.shape[1]), F32)
    return jnp.concatenate([top, gap, bottom, gap], axis=0)


def packed(real, imag):
    gap = jnp.zeros((real.shape[0], HALF - real.shape[1]), F32)
    return jnp.concatenate([real, gap, imag, gap], axis=1)


def charge_form(density):
    square = density.shape
    row, lane = rows(square), lanes(square)
    upper = jnp.where(row < lane, 2.0 * density, jnp.where(row == lane, density, 0.0))
    lower = jnp.where(row > lane, 2.0 * density, 0.0)
    cross = lower - jnp.transpose(lower)
    first = jnp.concatenate([upper, jnp.zeros(square, F32)], axis=1)
    return jnp.concatenate([first, jnp.concatenate([cross, upper], axis=1)], axis=0)


def cycle_kernel(
    ka_count, freq_count, thermal,
    mult_ref, owner_ref, energy_ref, proj_ref, self_ref, rotation_ref, orbital_ref,
    green_ref, slab_ref,
    columns, high, low, density_out, density_in, sums, half_in, half, chip_in, gathered,
    rates, charge_out, charge_in,
    orbital_sem, density_sem, half_sem, chip_sem, gather_sem, forward_sem, charge_sem,
):
    me, freq_me = lax.axis_index("ka"), lax.axis_index("freq")
    core, chip = lax.rem(me, 2), me // 2
    partner = me + 1 - 2 * core
    slots, orbs = self_ref.shape[0], self_ref.shape[2]
    bands = energy_ref.shape[1]
    slabs = columns.shape[0] // (2 * bands)
    owner_chips, _, each, _, wide = sums.shape
    chips = ka_count // 2
    full = owner_chips == chips
    weight = mult_ref[0].astype(F32)

    def when_owner(index, action):
        if full:
            action()
        else:
            pl.when(index < owner_chips)(action)

    def owned_chip(index):
        return index if full else jnp.minimum(index, owner_chips - 1)

    def remote(source, target, sems, at, **where):
        return pltpu.make_async_remote_copy(
            src_ref=source, dst_ref=target, send_sem=sems.at[0, at], recv_sem=sems.at[1, at],
            device_id=where, device_id_type=MESH,
        )

    load = pltpu.make_async_copy(orbital_ref, columns, orbital_sem)
    load.start()
    barrier = pltpu.get_barrier_semaphore()
    for j in range(1, ka_count):
        pl.semaphore_signal(barrier, inc=1, device_id={"ka": lax.rem(me + j, ka_count)}, device_id_type=MESH)
    for j in range(1, freq_count):
        pl.semaphore_signal(
            barrier, inc=1, device_id={"freq": lax.rem(freq_me + j, freq_count)}, device_id_type=MESH
        )

    across_re, across_im = proj_ref[0, 0], proj_ref[0, 1]
    pair = jnp.transpose(tall(across_re, across_im))
    swapped = swap(pair)
    weights_pp = split(jnp.concatenate([pair, swapped], axis=0))
    energy = energy_ref[...]
    energy_col = jnp.transpose(jnp.broadcast_to(energy, (bands, bands)))
    lane = lanes((orbs, wide))
    unit = jnp.where(lane == rows((orbs, wide)), 1.0, 0.0).astype(F32)

    def green_part(at):
        omega = [(2 * (q * freq_count + freq_me) + 1).astype(F32) * (math.pi * thermal) for q in at]
        inv = [1.0 / (w * w + energy * energy) for w in omega]
        bare_re = [-energy * v for v in inv]
        bare_im = [-w * v for w, v in zip(omega, inv)]
        c_re = [across_re * r + across_im * i for r, i in zip(bare_re, bare_im)]
        c_im = [across_re * i - across_im * r for r, i in zip(bare_re, bare_im)]
        g = [dot3(split(jnp.concatenate([a, b], axis=1)), weights_pp) for a, b in zip(c_re, c_im)]
        s = [split(packed(self_ref[q, 0], self_ref[q, 1])) for q in at]
        first = [
            split(tall(jnp.concatenate([a, b, c], axis=1), jnp.concatenate([-b, a, swap(c)], axis=1)))
            for a, b, c in zip(c_re, c_im, g)
        ]
        out = [dot3(a, b) for a, b in zip(s, first)]
        sc_re = [o[:, :bands] for o in out]
        sc_im = [o[:, bands : 2 * bands] for o in out]
        a1 = [o[:, 2 * bands :] for o in out]
        real_a = [split(tall(a, swap(a))) for a in a1]
        a2 = [dot3(split(a), r) for a, r in zip(a1, real_a)]
        a3 = [dot3(split(a), r) for a, r in zip(a2, real_a)]
        h = [a + b + c for a, b, c in zip(a1, a2, a3)]
        poly = [unit + a + dot3(split(a), split(tall(b, swap(b)))) for a, b in zip(h, a3)]
        real_sc = [
            split(tall(jnp.concatenate([a, b], axis=1), jnp.concatenate([-b, a], axis=1)))
            for a, b in zip(sc_re, sc_im)
        ]
        poly = [split(p) for p in poly]
        wg = [dot3(p, r) for p, r in zip(poly, real_a)]
        for q, one_g, one_w in zip(at, g, wg):
            one = weight * (one_g + dot3(split(one_g), split(tall(one_w, swap(one_w)))))
            place = (q // (2 * each), (q // each) % 2, q % each)
            sums[place] = jnp.where(lane >= HALF + orbs, weight, one)
        gain = None
        for w, p, r in zip(omega, poly, real_sc):
            one_v = dot3(p, r)
            inv_col = 1.0 / (w * w + energy_col * energy_col)
            left = split(pair * (-energy_col * inv_col) + swapped * (-w * inv_col))
            v_re, v_im = one_v[:, :bands], one_v[:, bands:]
            right = split(tall(one_v, jnp.concatenate([-v_im, v_re], axis=1)))
            term = dot3(left, right)
            gain = term if gain is None else gain + term
        return gain

    part_chips = owner_chips // PARTS
    half_copies, gain = [], None
    for part in range(PARTS):
        per = slots // PARTS
        one = green_part([part * per + g for g in range(per)])
        gain = one if gain is None else gain + one
        if part == 0:
            pl.semaphore_wait(barrier, ka_count + freq_count - 2)
        chunk = pl.ds(part * part_chips, part_chips)
        half_copies.append(remote(sums.at[chunk, 1 - core], half_in.at[chunk], half_sem, part, ka=partner))
        half_copies[-1].start()

    e_re, e_im = gain[:, :bands], gain[:, bands:]
    d_re = thermal * (e_re + jnp.transpose(e_re))
    d_im = thermal * (e_im - jnp.transpose(e_im))
    square = (bands, bands)
    density_out[...] = jnp.where(rows(square) <= lanes(square), d_re, d_im)
    density_copies = []
    for j in range(1, freq_count):
        density_copies.append(
            remote(density_out, density_in.at[j - 1], density_sem, j - 1, freq=lax.rem(freq_me + j, freq_count))
        )
        density_copies[-1].start()

    for part in range(PARTS):
        half_copies[part].wait_recv()
        for c in range(part * part_chips, (part + 1) * part_chips):
            half[c] = sums[c, core] + half_in[c]
    chip_copies = []
    for j in range(1, chips):
        to = lax.rem(chip + j, chips)
        copy = remote(half.at[owned_chip(to)], chip_in.at[j - 1], chip_sem, j - 1, ka=to * 2 + core)
        chip_copies.append((copy, to))
        when_owner(to, copy.start)

    load.wait()
    for s in range(slabs):
        high[s], low[s] = split(columns[pl.ds(s, 2 * bands, stride=slabs), :])

    for copy in density_copies:
        copy.wait()
    density = density_out[...]
    for j in range(1, freq_count):
        density = density + density_in[j - 1]
    form = split(charge_form(density))
    for s in range(slabs):
        product = dot3(form, (high[s], low[s]))
        one = high[s].astype(F32) + low[s].astype(F32)
        rates[pl.ds(s, 1), :] = weight * jnp.sum(product * one, axis=0, keepdims=True)
    selector = jnp.where(owner_ref[...] == rows((slabs, slabs)), 1.0, 0.0).astype(F32)
    owned = exact_dot(selector, rates[...])
    for d in range(slabs):
        charge_out[d, 0:1, :] = owned[d : d + 1]
        charge_out[d, 1:2, :] = jnp.full((1, owned.shape[1]), weight, F32)
    charge_copies = []
    for j in range(1, ka_count):
        to = lax.rem(me + j, ka_count)
        charge_copies.append(remote(charge_out.at[to], charge_in.at[j - 1], charge_sem, j - 1, ka=to))
        charge_copies[-1].start()

    spot = owned_chip(chip)
    gather_copies = [
        remote(
            gathered.at[spot, core], gathered.at[spot, core], gather_sem, j - 1,
            ka=lax.rem(chip + j, chips) * 2 + core,
        )
        for j in range(1, chips)
    ]
    sources = [chip] + [lax.rem(chip + chips - j, chips) for j in range(1, chips)]
    forward_copies = [
        remote(
            gathered.at[owned_chip(source), core], gathered.at[owned_chip(source), core],
            forward_sem, j, ka=partner,
        )
        for j, source in enumerate(sources)
    ]

    def reduce_and_send():
        for copy, _ in chip_copies:
            copy.wait_recv()
        turn = rotation_ref[...]
        gap = jnp.zeros((orbs, HALF - orbs), F32)
        zero = jnp.zeros((orbs, HALF), F32)
        right = tall(jnp.concatenate([turn, gap, zero], axis=1), jnp.concatenate([zero, turn, gap], axis=1))
        left = jnp.transpose(turn)
        for e in range(each):
            acc = half[spot, e]
            for j in range(1, chips):
                acc = acc + chip_in[j - 1, e]
            share = acc / acc[:1, wide - 1 :]
            gathered[spot, core, e] = exact_dot(left, exact_dot(share, right))
        for copy in gather_copies:
            copy.start()
        forward_copies[0].start()

    when_owner(chip, reduce_and_send)
    for j in range(1, chips):

        def pass_on(j=j):
            gather_copies[j - 1].wait_recv()
            forward_copies[j].start()

        when_owner(sources[j], pass_on)
    for copy in charge_copies:
        copy.wait()
    acc = charge_out[me]
    for j in range(1, ka_count):
        acc = acc + charge_in[j - 1]
    slab_ref[...] = acc[0:1] / acc[1:2]
    for j in range(chips):
        when_owner(sources[j], forward_copies[j].wait)
    green_ref[...] = gathered[...]
    for copy in half_copies:
        copy.wait_send()
    for copy, to in chip_copies:
        when_owner(to, copy.wait_send)

    def sent():
        for copy in gather_copies:
            copy.wait_send()

    when_owner(chip, sent)


def finish_kernel(gathered_ref, slab_in_ref, green_ref, slab_ref):
    orbs = green_ref.shape[3]
    each = gathered_ref.shape[2]
    for q in range(green_ref.shape[0]):
        value = gathered_ref[q // (2 * each), (q // each) % 2, q % each]
        green_ref[q, 0] = value[:, :orbs]
        green_ref[q, 1] = pltpu.roll(value, HALF, 1)[:, :orbs]
    slab_ref[...] = slab_in_ref[...]


def local(energy, projector, self_energy, multiplicity, orbitals, owner, rotation):
    slots, orbs = self_energy.shape[0], self_energy.shape[2]
    bands = energy.shape[1]
    slab_count, point_count = orbitals.shape[3], orbitals.shape[4]
    freq_count, ka_count = lax.axis_size("freq"), lax.axis_size("ka")
    thermal = 0.25 / (slots * freq_count)
    vmem = pl.BlockSpec(memory_space=pltpu.VMEM)
    smem = pl.BlockSpec(memory_space=pltpu.SMEM)
    owner_chips = min(slots, ka_count) // 2
    each = slots // (2 * owner_chips)
    chips, others = ka_count // 2, max(freq_count - 1, 1)
    tile = (each, orbs, 2 * HALF)
    dma = pltpu.SemaphoreType.DMA
    columns = orbitals.reshape(2 * bands * slab_count, point_count)
    gathered, slab = pl.pallas_call(
        functools.partial(cycle_kernel, ka_count, freq_count, thermal),
        out_shape=(
            jax.ShapeDtypeStruct((owner_chips, 2) + tile, F32),
            jax.ShapeDtypeStruct((1, point_count), F32),
        ),
        in_specs=[smem, vmem, vmem, vmem, vmem, vmem, pl.BlockSpec(memory_space=pl.ANY)],
        out_specs=(vmem, vmem),
        scratch_shapes=[
            pltpu.VMEM(columns.shape, F32),
            pltpu.VMEM((slab_count, 2 * bands, point_count), BF16),
            pltpu.VMEM((slab_count, 2 * bands, point_count), BF16),
            pltpu.VMEM((bands, bands), F32),
            pltpu.VMEM((others, bands, bands), F32),
            pltpu.VMEM((owner_chips, 2) + tile, F32),
            pltpu.VMEM((owner_chips,) + tile, F32),
            pltpu.VMEM((owner_chips,) + tile, F32),
            pltpu.VMEM((chips - 1,) + tile, F32),
            pltpu.VMEM((owner_chips, 2) + tile, F32),
            pltpu.VMEM((slab_count, point_count), F32),
            pltpu.VMEM((slab_count, 2, point_count), F32),
            pltpu.VMEM((ka_count - 1, 2, point_count), F32),
            dma,
            dma((2, others)),
            dma((2, PARTS)),
            dma((2, chips - 1)),
            dma((2, chips - 1)),
            dma((2, chips)),
            dma((2, ka_count - 1)),
        ],
        compiler_params=pltpu.CompilerParams(collective_id=0, has_side_effects=True),
        name="cycle",
    )(
        multiplicity, owner.reshape(1, slab_count), energy, jnp.swapaxes(projector, 2, 3),
        self_energy, rotation, columns,
    )
    return pl.pallas_call(
        finish_kernel,
        out_shape=(
            jax.ShapeDtypeStruct((slots, 2, orbs, orbs), F32),
            jax.ShapeDtypeStruct((1, point_count), F32),
        ),
        in_specs=[vmem, vmem],
        out_specs=(vmem, vmem),
        name="finish",
    )(gathered, slab)


def solution(mesh):
    in_specs = (
        P("ka", None),
        P("ka", None, None, None),
        P("freq", None, None, None),
        P("ka"),
        P("ka", None, None, None, "freq"),
        P(),
        P(),
    )
    out_specs = (P("freq", None, None, None), P("ka", "freq"))
    return jax.shard_map(local, mesh=mesh, in_specs=in_specs, out_specs=out_specs, check_vma=False)
```

```python
import functools
import math

import jax
import jax.numpy as jnp
from jax import lax
from jax.experimental import pallas as pl
from jax.experimental.pallas import tpu as pltpu
from jax.sharding import PartitionSpec as P

NS_STEPS = 3
PARTS = 2
EARLY = 4
HALF = 64
F32 = jnp.float32
BF16 = jnp.bfloat16
MESH = pl.DeviceIdType.MESH


def split(value):
    high = value.astype(BF16)
    return high, (value - high.astype(F32)).astype(BF16)


def dot3(first, second):
    one = functools.partial(jnp.dot, preferred_element_type=F32)
    return one(first[0], second[0]) + (one(first[1], second[0]) + one(first[0], second[1]))


def lanes(shape):
    return lax.broadcasted_iota(jnp.int32, shape, len(shape) - 1)


def rows(shape):
    return lax.broadcasted_iota(jnp.int32, shape, 0)


def swap(pair):
    turned = pltpu.roll(pair, HALF, 1)
    return jnp.where(lanes(pair.shape) < HALF, -turned, turned)


def tall(top, bottom):
    gap = jnp.zeros((HALF - top.shape[0], top.shape[1]), F32)
    return jnp.concatenate([top, gap, bottom, gap], axis=0)


def packed(real, imag):
    gap = jnp.zeros((real.shape[0], HALF - real.shape[1]), F32)
    return jnp.concatenate([real, gap, imag, gap], axis=1)


def charge_form(density):
    square = density.shape
    row, lane = rows(square), lanes(square)
    upper = jnp.where(row < lane, 2.0 * density, jnp.where(row == lane, density, 0.0))
    lower = jnp.where(row > lane, 2.0 * density, 0.0)
    cross = lower - jnp.transpose(lower)
    first = jnp.concatenate([upper, jnp.zeros(square, F32)], axis=1)
    return jnp.concatenate([first, jnp.concatenate([cross, upper], axis=1)], axis=0)


def cycle_kernel(
    ka_count, freq_count, thermal,
    mult_ref, owner_ref, energy_ref, proj_ref, self_hbm, rotation_ref, orbital_ref,
    green_ref, slab_ref,
    self_ref, columns, high, low, coupled, series, density_out, density_in, sums, half_in, half, chip_in, gathered,
    rates, charge_out, charge_in,
    self_sem, orbital_sem, density_sem, half_sem, chip_sem, gather_sem, forward_sem, charge_sem,
):
    me, freq_me = lax.axis_index("ka"), lax.axis_index("freq")
    core, chip = lax.rem(me, 2), me // 2
    partner = me + 1 - 2 * core
    slots, orbs = self_ref.shape[0], self_ref.shape[2]
    bands = energy_ref.shape[1]
    slabs, points = columns.shape[0] // (2 * bands), columns.shape[1]
    owner_chips, _, each, _, wide = sums.shape
    chips = ka_count // 2
    full = owner_chips == chips
    weight = mult_ref[0].astype(F32)

    def when_owner(index, action):
        if full:
            action()
        else:
            pl.when(index < owner_chips)(action)

    def owned_chip(index):
        return index if full else jnp.minimum(index, owner_chips - 1)

    def remote(source, target, sems, at, **where):
        return pltpu.make_async_remote_copy(
            src_ref=source, dst_ref=target, send_sem=sems.at[0, at], recv_sem=sems.at[1, at],
            device_id=where, device_id_type=MESH,
        )

    fetch = pltpu.make_async_copy(self_hbm, self_ref, self_sem)
    fetch.start()
    load = pltpu.make_async_copy(orbital_ref, columns, orbital_sem)
    load.start()
    barrier = pltpu.get_barrier_semaphore()
    for j in range(1, ka_count):
        pl.semaphore_signal(barrier, inc=1, device_id={"ka": lax.rem(me + j, ka_count)}, device_id_type=MESH)
    for j in range(1, freq_count):
        pl.semaphore_signal(
            barrier, inc=1, device_id={"freq": lax.rem(freq_me + j, freq_count)}, device_id_type=MESH
        )

    across_re, across_im = proj_ref[0, 0], proj_ref[0, 1]
    pair = jnp.transpose(tall(across_re, across_im))
    swapped = swap(pair)
    weights_pp = split(jnp.concatenate([pair, swapped], axis=0))
    energy = energy_ref[...]
    energy_col = jnp.transpose(jnp.broadcast_to(energy, (bands, bands)))
    lane = lanes((orbs, wide))
    unit = jnp.where(lane == rows((orbs, wide)), 1.0, 0.0).astype(F32)

    def omega_of(q):
        return (2 * (q * freq_count + freq_me) + 1).astype(F32) * (math.pi * thermal)

    def real_wide(value):
        re, im = value[:, :bands], value[:, bands:]
        return split(tall(value, jnp.concatenate([-im, re], axis=1)))

    def green_part(at):
        omega = [omega_of(q) for q in at]
        inv = [1.0 / (w * w + energy * energy) for w in omega]
        bare_re = [-energy * v for v in inv]
        bare_im = [-w * v for w, v in zip(omega, inv)]
        c_re = [across_re * r + across_im * i for r, i in zip(bare_re, bare_im)]
        c_im = [across_re * i - across_im * r for r, i in zip(bare_re, bare_im)]
        g = [dot3(split(jnp.concatenate([a, b], axis=1)), weights_pp) for a, b in zip(c_re, c_im)]
        s = [split(packed(self_ref[q, 0], self_ref[q, 1])) for q in at]
        first = [
            split(tall(jnp.concatenate([a, b, c], axis=1), jnp.concatenate([-b, a, swap(c)], axis=1)))
            for a, b, c in zip(c_re, c_im, g)
        ]
        out = [dot3(a, b) for a, b in zip(s, first)]
        a1 = [o[:, 2 * bands :] for o in out]
        real_a = [split(tall(a, swap(a))) for a in a1]
        a2 = [dot3(split(a), r) for a, r in zip(a1, real_a)]
        a3 = [dot3(split(a), r) for a, r in zip(a2, real_a)]
        h = [a + b + c for a, b, c in zip(a1, a2, a3)]
        poly = [unit + a + dot3(split(a), split(tall(b, swap(b)))) for a, b in zip(h, a3)]
        for q, o, p in zip(at, out, poly):
            coupled[q], series[q] = o[:, : 2 * bands], p
        poly = [split(p) for p in poly]
        wg = [dot3(p, r) for p, r in zip(poly, real_a)]
        for q, one_g, one_w in zip(at, g, wg):
            one = weight * (one_g + dot3(split(one_g), split(tall(one_w, swap(one_w)))))
            place = (q // (2 * each), (q // each) % 2, q % each)
            sums[place] = jnp.where(lane >= HALF + orbs, weight, one)

    def density_part(at):
        gain = None
        for q in at:
            w = omega_of(q)
            one_v = dot3(split(series[q]), real_wide(coupled[q]))
            inv_col = 1.0 / (w * w + energy_col * energy_col)
            left = split(pair * (-energy_col * inv_col) + swapped * (-w * inv_col))
            term = dot3(left, real_wide(one_v))
            gain = term if gain is None else gain + term
        return gain

    part_chips = owner_chips // PARTS
    half_copies, gain = [], 0.0
    per = slots // PARTS
    fetch.wait()
    for part in range(PARTS):
        green_part([part * per + g for g in range(per)])
        if part > 0:
            gain = gain + density_part(range((part - 1) * per, part * per))
        if part == 0:
            pl.semaphore_wait(barrier, ka_count + freq_count - 2)
        chunk = pl.ds(part * part_chips, part_chips)
        half_copies.append(remote(sums.at[chunk, 1 - core], half_in.at[chunk], half_sem, part, ka=partner))
        half_copies[-1].start()

    chip_copies = []
    for part in range(PARTS):
        half_copies[part].wait_recv()
        for c in range(part * part_chips, (part + 1) * part_chips):
            half[c] = sums[c, core] + half_in[c]
        for j in range(1, chips):
            to = lax.rem(chip + j, chips)
            copy = remote(half.at[owned_chip(to)], chip_in.at[j - 1], chip_sem, j - 1, ka=to * 2 + core)
            if part == 0:
                chip_copies.append((copy, to))
            inside = jnp.logical_and(to >= part * part_chips, to < (part + 1) * part_chips)
            pl.when(inside)(copy.start)
        if part == PARTS - 2:
            gain = gain + density_part(range(slots - per, slots - per + per // EARLY))
    gain = gain + density_part(range(slots - per + per // EARLY, slots))
    e_re, e_im = gain[:, :bands], gain[:, bands:]
    d_re = thermal * (e_re + jnp.transpose(e_re))
    d_im = thermal * (e_im - jnp.transpose(e_im))
    square = (bands, bands)
    density_out[...] = jnp.where(rows(square) <= lanes(square), d_re, d_im)
    density_copies = []
    for j in range(1, freq_count):
        density_copies.append(
            remote(density_out, density_in.at[j - 1], density_sem, j - 1, freq=lax.rem(freq_me + j, freq_count))
        )
        density_copies[-1].start()

    load.wait()
    for s in range(slabs):
        place = pl.ds((s % 2) * points, points)
        high[s // 2, :, place], low[s // 2, :, place] = split(columns[pl.ds(s, 2 * bands, stride=slabs), :])

    spot = owned_chip(chip)
    gather_copies = [
        remote(
            gathered.at[spot, core], gathered.at[spot, core], gather_sem, j - 1,
            ka=lax.rem(chip + j, chips) * 2 + core,
        )
        for j in range(1, chips)
    ]
    sources = [chip] + [lax.rem(chip + chips - j, chips) for j in range(1, chips)]
    forward_copies = [
        remote(
            gathered.at[owned_chip(source), core], gathered.at[owned_chip(source), core],
            forward_sem, j, ka=partner,
        )
        for j, source in enumerate(sources)
    ]

    def reduce_and_send():
        for copy, _ in chip_copies:
            copy.wait_recv()
        turn = rotation_ref[...]
        gap = jnp.zeros((orbs, HALF - orbs), F32)
        zero = jnp.zeros((orbs, HALF), F32)
        right = tall(jnp.concatenate([turn, gap, zero], axis=1), jnp.concatenate([zero, turn, gap], axis=1))
        left = split(jnp.transpose(turn))
        right = split(right)
        for e in range(each):
            acc = half[spot, e]
            for j in range(1, chips):
                acc = acc + chip_in[j - 1, e]
            share = acc / acc[:1, wide - 1 :]
            gathered[spot, core, e] = dot3(left, split(dot3(split(share), right)))
        for copy in gather_copies:
            copy.start()
        forward_copies[0].start()

    when_owner(chip, reduce_and_send)
    for copy in density_copies:
        copy.wait()
    density = density_out[...]
    for j in range(1, freq_count):
        density = density + density_in[j - 1]
    form = split(charge_form(density))
    for s in range(slabs // 2):
        one = (high[s], low[s])
        product = dot3(form, one) * (one[0].astype(F32) + one[1].astype(F32))
        rate = weight * jnp.sum(product, axis=0, keepdims=True)
        rates[pl.ds(2 * s, 1), :], rates[pl.ds(2 * s + 1, 1), :] = rate[:, :points], rate[:, points:]
    selector = jnp.where(owner_ref[...] == rows((slabs, slabs)), 1.0, 0.0).astype(F32)
    parted = split(rates[...])
    owned = jnp.dot(selector.astype(BF16), parted[0], preferred_element_type=F32)
    owned = owned + jnp.dot(selector.astype(BF16), parted[1], preferred_element_type=F32)
    for d in range(slabs):
        charge_out[d, 0:1, :] = owned[d : d + 1]
        charge_out[d, 1:2, :] = jnp.full((1, owned.shape[1]), weight, F32)
    charge_copies = []
    for j in range(1, ka_count):
        to = lax.rem(me + j, ka_count)
        charge_copies.append(remote(charge_out.at[to], charge_in.at[j - 1], charge_sem, j - 1, ka=to))
        charge_copies[-1].start()

    for j in range(1, chips):

        def pass_on(j=j):
            gather_copies[j - 1].wait_recv()
            forward_copies[j].start()

        when_owner(sources[j], pass_on)
    for copy in charge_copies:
        copy.wait()
    acc = charge_out[me]
    for j in range(1, ka_count):
        acc = acc + charge_in[j - 1]
    slab_ref[...] = acc[0:1] / acc[1:2]
    for j in range(chips):
        when_owner(sources[j], forward_copies[j].wait)
    green_ref[...] = gathered[...]
    for copy in half_copies:
        copy.wait_send()
    for copy, to in chip_copies:
        when_owner(to, copy.wait_send)

    def sent():
        for copy in gather_copies:
            copy.wait_send()

    when_owner(chip, sent)


def finish_kernel(gathered_ref, slab_in_ref, green_ref, slab_ref):
    orbs = green_ref.shape[3]
    each = gathered_ref.shape[2]
    for q in range(green_ref.shape[0]):
        value = gathered_ref[q // (2 * each), (q // each) % 2, q % each]
        green_ref[q, 0] = value[:, :orbs]
        green_ref[q, 1] = pltpu.roll(value, HALF, 1)[:, :orbs]
    slab_ref[...] = slab_in_ref[...]


def local(energy, projector, self_energy, multiplicity, orbitals, owner, rotation):
    slots, orbs = self_energy.shape[0], self_energy.shape[2]
    bands = energy.shape[1]
    slab_count, point_count = orbitals.shape[3], orbitals.shape[4]
    freq_count, ka_count = lax.axis_size("freq"), lax.axis_size("ka")
    thermal = 0.25 / (slots * freq_count)
    vmem = pl.BlockSpec(memory_space=pltpu.VMEM)
    smem = pl.BlockSpec(memory_space=pltpu.SMEM)
    hbm = pl.BlockSpec(memory_space=pl.ANY)
    owner_chips = min(slots, ka_count) // 2
    each = slots // (2 * owner_chips)
    chips, others = ka_count // 2, max(freq_count - 1, 1)
    tile = (each, orbs, 2 * HALF)
    dma = pltpu.SemaphoreType.DMA
    columns = orbitals.reshape(2 * bands * slab_count, point_count)
    gathered, slab = pl.pallas_call(
        functools.partial(cycle_kernel, ka_count, freq_count, thermal),
        out_shape=(
            jax.ShapeDtypeStruct((owner_chips, 2) + tile, F32),
            jax.ShapeDtypeStruct((1, point_count), F32),
        ),
        in_specs=[smem, vmem, vmem, vmem, hbm, vmem, hbm],
        out_specs=(vmem, vmem),
        scratch_shapes=[
            pltpu.VMEM(self_energy.shape, F32),
            pltpu.VMEM(columns.shape, F32),
            pltpu.VMEM((slab_count // 2, 2 * bands, 2 * point_count), BF16),
            pltpu.VMEM((slab_count // 2, 2 * bands, 2 * point_count), BF16),
            pltpu.VMEM((slots, orbs, 2 * bands), F32),
            pltpu.VMEM((slots, orbs, 2 * HALF), F32),
            pltpu.VMEM((bands, bands), F32),
            pltpu.VMEM((others, bands, bands), F32),
            pltpu.VMEM((owner_chips, 2) + tile, F32),
            pltpu.VMEM((owner_chips,) + tile, F32),
            pltpu.VMEM((owner_chips,) + tile, F32),
            pltpu.VMEM((chips - 1,) + tile, F32),
            pltpu.VMEM((owner_chips, 2) + tile, F32),
            pltpu.VMEM((slab_count, point_count), F32),
            pltpu.VMEM((slab_count, 2, point_count), F32),
            pltpu.VMEM((ka_count - 1, 2, point_count), F32),
            dma,
            dma,
            dma((2, others)),
            dma((2, PARTS)),
            dma((2, chips - 1)),
            dma((2, chips - 1)),
            dma((2, chips)),
            dma((2, ka_count - 1)),
        ],
        compiler_params=pltpu.CompilerParams(collective_id=0, has_side_effects=True),
        name="cycle",
    )(
        multiplicity, owner.reshape(1, slab_count), energy, jnp.swapaxes(projector, 2, 3),
        self_energy, rotation, columns,
    )
    return pl.pallas_call(
        finish_kernel,
        out_shape=(
            jax.ShapeDtypeStruct((slots, 2, orbs, orbs), F32),
            jax.ShapeDtypeStruct((1, point_count), F32),
        ),
        in_specs=[vmem, vmem],
        out_specs=(vmem, vmem),
        name="finish",
    )(gathered, slab)


def solution(mesh):
    in_specs = (
        P("ka", None),
        P("ka", None, None, None),
        P("freq", None, None, None),
        P("ka"),
        P("ka", None, None, None, "freq"),
        P(),
        P(),
    )
    out_specs = (P("freq", None, None, None), P("ka", "freq"))
    return jax.shard_map(local, mesh=mesh, in_specs=in_specs, out_specs=out_specs, check_vma=False)
```
